32 devices in a mesh: grp: 4 (over y, x), blk: 8 (over z, core).
Axes of the slice: x: 2, y: 2, z: 4, core: 2. Of those that a mesh axis runs over, the one named last changes fastest.
Arguments:
- estimate: float32 [32, 256, 256], P('blk'), may hold values from 0.25 to 4
- measured: bfloat16 [6, 256, 32, 256], P(None, 'blk'), may hold values from 0.25 to 4
- tile_plane: int32 [6, 256], P(None, 'blk'), may hold values from 0 to 31, as said below
- tile_strip: int32 [6, 256], P(None, 'blk'), may hold values from 0 to 7, as said below
- view_group: int32 [6], replicated, may hold values from 0 to 3, as said below
- kernel_cols: float32 [6, 3, 31], replicated, may hold values from 0.002 to 0.1
- kernel_rows: float32 [6, 3, 31], replicated, may hold values from 0.002 to 0.1
- kernel_planes: float32 [6, 3, 31], replicated, may hold values from 0.002 to 0.1
Outputs:
- updated: float32 [32, 256, 256], P('blk')
The draws below stay inside these ranges and needn't reach their ends.
Inputs may be any that keep to these rules, and one draw needn't show every extreme that they name: For each view the pairs (tile_plane, tile_strip) name every plane and strip exactly once; the 32 tiles of one view on one device of blk hold exactly 4 tiles of every block of 4 consecutive planes and exactly 4 tiles of every strip. `tile_strip`: see tile_plane. `view_group`: every group has at least one view and at most 2; some group has exactly 2.
All inputs are finite; a program needn't handle non-finite values.
Results may differ from the reference program's by a relative error of at most 0.0003.
Values may be sent and summed in bfloat16 or wider, within the bound.
A program may use at most 128 MiB of HBM per device.

```python
import math
import jax
import jax.numpy as jnp
from jax import lax

NX = 256
NY = 256
CZ = 4
VIEWS = 6
RANK = 3
TAPS = 31
NZ = 32
PY = 32
TILES = 256
N_GRP = 4
N_BLK = 8


def tile_layout(key):
    holders = N_BLK
    listing = []
    for view in range(VIEWS):
        view_key = jax.random.fold_in(key, view)
        sigma = jax.random.permutation(jax.random.fold_in(view_key, 1), holders)
        shuffle = jax.random.permutation(jax.random.fold_in(view_key, 2), holders)
        inverse = jnp.zeros((holders,), jnp.int32).at[shuffle].set(jnp.arange(holders, dtype=jnp.int32))
        holder = jnp.arange(holders, dtype=jnp.int32)[:, None]
        owner = jnp.arange(holders, dtype=jnp.int32)[None, :]
        strip = inverse[(holder - sigma[owner]) % holders]
        plane = owner[:, :, None] * CZ + jnp.arange(CZ, dtype=jnp.int32)[None, None, :]
        ident = (plane * holders + strip[:, :, None]).reshape(holders, holders * CZ)
        ident = jax.random.permutation(jax.random.fold_in(view_key, 3), ident, axis=1, independent=True)
        listing.append(ident.reshape(-1))
    return jnp.stack(listing).astype(jnp.int32)


def draw_tile_plane(key, part):
    return (tile_layout(key) // N_BLK).astype(jnp.int32)


def draw_tile_strip(key, part):
    return (tile_layout(key) % N_BLK).astype(jnp.int32)


def draw_view_group(key, part):
    base = jnp.arange(VIEWS, dtype=jnp.int32) % N_GRP
    relabel = jax.random.permutation(jax.random.fold_in(key, 11), N_GRP).astype(jnp.int32)
    return jax.random.permutation(jax.random.fold_in(key, 12), relabel[base]).astype(jnp.int32)


def level_of(stream_key, shape, shards, low, largest):
    loudness, own = 1.0, jax.random.fold_in(stream_key, 6)
    for dim, shards_of in shards:
        draws = jnp.exp(jax.random.uniform(jax.random.fold_in(own, dim), (shards_of,), jnp.float32, low / len(shards), largest / len(shards)))
        loudness = loudness * jnp.repeat(draws, shape[dim] // shards_of).reshape([-1 if axis == dim else 1 for axis in range(len(shape))])
    return loudness


def setup_inputs(seed: int = 0) -> dict:
    streams_of = jax.random.split(jax.random.key(seed), 9)
    estimate = jnp.clip(jnp.exp(math.log(4.0) - 2.7725887 * jax.random.uniform(streams_of[0], (NZ, NY, NX), jnp.float32) ** level_of(streams_of[0], (NZ, NY, NX), ((0, 8),), -0.2, 0.2)), 0.25, 4.0)
    measured = jnp.clip(jnp.exp(math.log(4.0) - 2.7725887 * jax.random.uniform(streams_of[1], (VIEWS, TILES, PY, NX), jnp.float32) ** level_of(streams_of[1], (VIEWS, TILES, PY, NX), ((1, 8),), -0.2, 0.2)), 0.25, 4.0).astype(jnp.bfloat16)
    tile_plane = draw_tile_plane(jax.random.fold_in(streams_of[8], 71), 0)
    tile_strip = draw_tile_strip(jax.random.fold_in(streams_of[8], 71), 0)
    view_group = draw_view_group(jax.random.fold_in(streams_of[8], 71), 0)
    kernel_cols = jnp.clip(jnp.exp(jax.random.uniform(streams_of[5], (VIEWS, RANK, TAPS), jnp.float32, math.log(0.002), math.log(0.1))), 0.002, 0.1)
    kernel_rows = jnp.clip(jnp.exp(jax.random.uniform(streams_of[6], (VIEWS, RANK, TAPS), jnp.float32, math.log(0.002), math.log(0.1))), 0.002, 0.1)
    kernel_planes = jnp.clip(jnp.exp(jax.random.uniform(streams_of[7], (VIEWS, RANK, TAPS), jnp.float32, math.log(0.002), math.log(0.1))), 0.002, 0.1)
    return {"estimate": estimate, "measured": measured, "tile_plane": tile_plane, "tile_strip": tile_strip, "view_group": view_group, "kernel_cols": kernel_cols, "kernel_rows": kernel_rows, "kernel_planes": kernel_planes}


def banded(taps, length):
    width = taps.shape[-1]
    half = width // 2
    position = jnp.arange(length, dtype=jnp.int32)
    offsets = position[None, :] - position[:, None] + half
    onehot = (offsets[:, :, None] == jnp.arange(width, dtype=jnp.int32)[None, None, :]).astype(jnp.float32)
    return jnp.einsum("imt,rt->rim", onehot, taps, precision=lax.Precision.HIGHEST)


def reference(estimate, measured, tile_plane, tile_strip, view_group, kernel_cols, kernel_rows, kernel_planes):
    highest = lax.Precision.HIGHEST
    group_sums = jnp.zeros((N_GRP, NZ, NY, NX), jnp.float32)
    group_sizes = jnp.zeros((N_GRP,), jnp.float32)
    for view in range(VIEWS):
        positions = (tile_plane[view] * N_BLK + tile_strip[view]).astype(jnp.int32)
        observed = jnp.zeros((NZ * N_BLK, PY, NX), jnp.bfloat16).at[positions].set(measured[view]).reshape(NZ, NY, NX)
        band_cols = banded(kernel_cols[view], NX)
        band_rows = banded(kernel_rows[view], NY)
        band_planes = banded(kernel_planes[view], NZ)
        rank_terms = jnp.einsum("zym,rim->rzyi", estimate, band_cols, precision=highest)
        rank_terms = jnp.einsum("rzmx,rim->rzix", rank_terms, band_rows, precision=highest)
        blurred = jnp.einsum("rmyx,rim->iyx", rank_terms, band_planes, precision=highest)
        ratios = observed.astype(jnp.float32) / blurred
        adjoint = jnp.einsum("iyx,rim->rmyx", ratios, band_planes, precision=highest)
        adjoint = jnp.einsum("rzix,rim->rzmx", adjoint, band_rows, precision=highest)
        factor = jnp.einsum("rzyi,rim->zym", adjoint, band_cols, precision=highest)
        membership = (view_group[view] == jnp.arange(N_GRP, dtype=jnp.int32)).astype(jnp.float32)
        group_sums = group_sums + membership[:, None, None, None] * factor[None]
        group_sizes = group_sizes + membership
    log_mean = jnp.sum(jnp.log(group_sums / group_sizes[:, None, None, None]), axis=0)
    return estimate * jnp.exp(log_mean / N_GRP)
```

```python
import jax
import jax.numpy as jnp
from jax import lax
from jax.sharding import PartitionSpec as P

VSLOT = 2
HIGH = lax.Precision.HIGH


def band(taps, rows, cols, lead):
    width = taps.shape[-1]
    shift = lax.broadcasted_iota(jnp.int32, (rows, cols), 1) - lax.broadcasted_iota(
        jnp.int32, (rows, cols), 0
    )
    shift = shift - lead + width // 2
    out = jnp.zeros(taps.shape[:-1] + (rows, cols), jnp.float32)
    for t in range(width):
        out = jnp.where(shift == t, taps[..., t, None, None], out)
    return out


def shards(estimate, measured, tile_plane, tile_strip, view_group, kernel_cols, kernel_rows, kernel_planes):
    cz, ny, nx = estimate.shape
    blocks = lax.axis_size("blk")
    groups = lax.axis_size("grp")
    nz = cz * blocks
    py = ny // blocks
    half = kernel_rows.shape[-1] // 2
    lead = -(-half // 8) * 8
    ext = py + 2 * lead
    tiles = measured.shape[1]
    per = tiles // blocks

    matches = (view_group == lax.axis_index("grp")).astype(jnp.int32)
    ranking = jnp.cumsum(matches) - matches
    members = jnp.sum(matches).astype(jnp.float32)
    ids = jnp.arange(view_group.shape[0], dtype=jnp.int32)
    picked = [matches * (ranking == s).astype(jnp.int32) for s in range(VSLOT)]
    chosen = [jnp.sum(p * ids) for p in picked]
    weights = jnp.stack([jnp.sum(p).astype(jnp.float32) / members for p in picked])

    padded = jnp.pad(estimate, ((0, 0), (lead, lead), (0, 0)))
    windows = jnp.stack([padded[:, j * py : j * py + ext] for j in range(blocks)])
    pencil = lax.all_to_all(windows, "blk", 0, 0, tiled=True).reshape(nz, ext, nx)

    pick = lambda a: jnp.stack([lax.dynamic_index_in_dim(a, c, 0, keepdims=False) for c in chosen])
    pieces, planes, strips = pick(measured), pick(tile_plane), pick(tile_strip)
    hits = (strips[:, :, None] == jnp.arange(blocks, dtype=jnp.int32)).astype(jnp.int32)
    before = jnp.cumsum(hits, axis=1) - hits
    positions = strips * per + jnp.sum(before * hits, axis=2)
    order = positions[:, None, :] == jnp.arange(tiles, dtype=jnp.int32)[None, :, None]
    send_planes = jnp.sum(jnp.where(order, planes[:, None, :], 0), axis=2)
    send = jnp.einsum("vpi,viyx->pvyx", order.astype(jnp.bfloat16), pieces)
    got = lax.all_to_all(send, "blk", 0, 0, tiled=True)
    got_planes = lax.all_to_all(send_planes.T, "blk", 0, 0, tiled=True)
    place = (got_planes[None] == jnp.arange(nz, dtype=jnp.int32)[:, None, None]).astype(jnp.bfloat16)
    observed = jnp.einsum("ptv,tvyx->vpyx", place, got).astype(jnp.float32)

    kc, kr, kp = pick(kernel_cols), pick(kernel_rows), pick(kernel_planes)
    bx = band(kc, nx, nx, 0)
    by = band(kr, py, ext, lead)
    bz = band(kp, nz, nz, 0)
    byw = by * weights[:, None, None, None]

    t = jnp.einsum("zmx,vrim->vrzix", pencil, by, precision=HIGH)
    t = jnp.einsum("vrzix,vrnx->vrzin", t, bx, precision=HIGH)
    blurred = jnp.einsum("vrzin,vrpz->vpin", t, bz, precision=HIGH)
    ratios = observed / blurred
    a = jnp.einsum("vpin,vrpz->vrzin", ratios, bz, precision=HIGH)
    a = jnp.einsum("vrzin,vrnx->vrzix", a, bx, precision=HIGH)
    wide = jnp.einsum("vrzix,vrim->zmx", a, byw, precision=HIGH)

    chunk = min(py, lead)
    average = wide[:, lead : lead + py]
    for d in range(1, lead // chunk + 1):
        up = wide[:, lead + py + (d - 1) * chunk : lead + py + d * chunk]
        down = wide[:, lead - d * chunk : lead - (d - 1) * chunk]
        up = lax.ppermute(up, "blk", [(i, i + d) for i in range(blocks - d)])
        down = lax.ppermute(down, "blk", [(i, i - d) for i in range(d, blocks)])
        rest = py - chunk
        average = average + jnp.pad(up, ((0, 0), (0, rest), (0, 0))) + jnp.pad(down, ((0, 0), (rest, 0), (0, 0)))
    logs = jnp.log(average)
    logs = lax.all_to_all(logs.reshape(blocks, cz, py, nx), "blk", 0, 0, tiled=True)
    summed = lax.psum(logs, "grp")
    summed = jnp.transpose(summed, (1, 0, 2, 3)).reshape(cz, ny, nx)
    return estimate * jnp.exp(summed / groups)


def solution(mesh):
    in_specs = (
        P("blk", None, None),
        P(None, "blk", None, None),
        P(None, "blk"),
        P(None, "blk"),
        P(),
        P(),
        P(),
        P(),
    )
    return jax.shard_map(
        shards, mesh=mesh, in_specs=in_specs, out_specs=P("blk", None, None), check_vma=False
    )
```

```python
import jax
import jax.numpy as jnp
from jax import lax
from jax.experimental import pallas as pl
from jax.experimental.pallas import tpu as pltpu
from jax.sharding import PartitionSpec as P

VSLOT = 2
HIGH = lax.Precision.HIGH


MESH = pl.DeviceIdType.MESH


def band_kernel(*refs):
    count = len(refs) // 2
    for row, out in zip(refs[:count], refs[count:]):
        number, rows, cols = out.shape
        for n in range(number):
            wide = jnp.broadcast_to(row[n], (rows, row.shape[-1]))
            wide = pltpu.roll(wide, 0, 1, stride=1, stride_axis=0)
            out[n] = wide[:, :cols]


def bands(shapes):
    rows_in, outs = [], []
    for taps, rows, cols, lead in shapes:
        number, width = taps.shape
        half = width // 2
        span = -(-(max(cols, rows) + lead + width) // 128) * 128
        row = jnp.pad(taps, ((0, 0), (0, span - width)))
        row = jnp.roll(row, lead - half, axis=1)
        rows_in.append(row[:, None, :])
        outs.append(jax.ShapeDtypeStruct((number, rows, cols), jnp.float32))
    vmem = pl.BlockSpec(memory_space=pltpu.VMEM)
    return pl.pallas_call(
        band_kernel,
        out_shape=outs,
        in_specs=[vmem] * len(outs),
        out_specs=[vmem] * len(outs),
    )(*rows_in)


def finish_kernel(blocks, groups, logs, est, out, got1, send2, got2, s1, r1, s2, r2, s3, r3):
    me = lax.axis_index("blk")
    grp = lax.axis_index("grp")
    cq = est.shape[0] // groups
    mine = pl.ds(grp * cq, cq)
    barrier = pltpu.get_barrier_semaphore()
    for k in range(1, groups):
        pl.semaphore_signal(barrier, inc=1, device_id=(lax.rem(grp + k, groups), me), device_id_type=MESH)
    for rel in range(1, blocks):
        pl.semaphore_signal(barrier, inc=1, device_id=(grp, lax.rem(me + rel, blocks)), device_id_type=MESH)
    pl.semaphore_wait(barrier, groups + blocks - 2)
    order = list(range(1, blocks)) + [0]

    first, second, third = {}, {}, {}
    for rel in order:
        dest = lax.rem(me + rel, blocks)
        for k in range(1, groups):
            peer = lax.rem(grp + k, groups)
            first[rel, k] = pltpu.make_async_remote_copy(
                src_ref=logs.at[dest, pl.ds(peer * cq, cq)],
                dst_ref=got1.at[rel, k - 1],
                send_sem=s1.at[rel, k - 1],
                recv_sem=r1.at[rel, k - 1],
                device_id=(peer, me),
                device_id_type=MESH,
            )
            first[rel, k].start()
    for rel in order:
        dest = lax.rem(me + rel, blocks)
        total = logs[dest, mine]
        for k in range(1, groups):
            first[rel, k].wait_recv()
            total = total + got1[rel, k - 1]
        if rel == 0:
            got2[0] = total
        else:
            send2[rel] = total
            second[rel] = pltpu.make_async_remote_copy(
                src_ref=send2.at[rel],
                dst_ref=got2.at[rel],
                send_sem=s2.at[rel],
                recv_sem=r2.at[rel],
                device_id=(grp, dest),
                device_id_type=MESH,
            )
            second[rel].start()
    for rel in order:
        strip = lax.rem(me + blocks - rel, blocks)
        if rel != 0:
            second[rel].wait_recv()
        out[mine, strip] = est[mine, strip] * jnp.exp(got2[rel] * (1.0 / groups))
        for k in range(1, groups):
            third[rel, k] = pltpu.make_async_remote_copy(
                src_ref=out.at[mine, strip],
                dst_ref=out.at[mine, strip],
                send_sem=s3.at[rel, k - 1],
                recv_sem=r3.at[rel, k - 1],
                device_id=(lax.rem(grp + k, groups), me),
                device_id_type=MESH,
            )
            third[rel, k].start()
    for copy in first.values():
        copy.wait_send()
    for copy in second.values():
        copy.wait_send()
    for copy in third.values():
        copy.wait_send()
    for rel in order:
        strip = lax.rem(me + blocks - rel, blocks)
        for k in range(1, groups):
            peer = lax.rem(grp + groups - k, groups)
            theirs = out.at[pl.ds(peer * cq, cq), strip]
            pltpu.make_async_remote_copy(
                src_ref=theirs,
                dst_ref=theirs,
                send_sem=s3.at[rel, k - 1],
                recv_sem=r3.at[rel, k - 1],
                device_id=(peer, me),
                device_id_type=MESH,
            ).wait_recv()


def finish(logs, estimate, blocks, groups):
    cz, ny, nx = estimate.shape
    py = ny // blocks
    cq = cz // groups
    vmem = pl.BlockSpec(memory_space=pltpu.VMEM)
    dma = pltpu.SemaphoreType.DMA
    out = pl.pallas_call(
        lambda *refs: finish_kernel(blocks, groups, *refs),
        out_shape=jax.ShapeDtypeStruct((cz, blocks, py, nx), jnp.float32),
        in_specs=[vmem, vmem],
        out_specs=vmem,
        scratch_shapes=[
            pltpu.VMEM((blocks, groups - 1, cq, py, nx), jnp.float32),
            pltpu.VMEM((blocks, cq, py, nx), jnp.float32),
            pltpu.VMEM((blocks, cq, py, nx), jnp.float32),
            dma((blocks, groups - 1)),
            dma((blocks, groups - 1)),
            dma((blocks,)),
            dma((blocks,)),
            dma((blocks, groups - 1)),
            dma((blocks, groups - 1)),
        ],
        compiler_params=pltpu.CompilerParams(collective_id=0, has_side_effects=True),
        name="finish",
    )(logs.reshape(blocks, cz, py, nx), estimate.reshape(cz, blocks, py, nx))
    return out.reshape(cz, ny, nx)


def shards(estimate, measured, tile_plane, tile_strip, view_group, kernel_cols, kernel_rows, kernel_planes):
    cz, ny, nx = estimate.shape
    blocks = lax.axis_size("blk")
    groups = lax.axis_size("grp")
    nz = cz * blocks
    py = ny // blocks
    half = kernel_rows.shape[-1] // 2
    lead = -(-half // 8) * 8
    ext = py + 2 * lead
    tiles = measured.shape[1]
    per = tiles // blocks

    matches = (view_group == lax.axis_index("grp")).astype(jnp.int32)
    ranking = jnp.cumsum(matches) - matches
    members = jnp.sum(matches).astype(jnp.float32)
    ids = jnp.arange(view_group.shape[0], dtype=jnp.int32)
    picked = [matches * (ranking == s).astype(jnp.int32) for s in range(VSLOT)]
    chosen = [jnp.sum(p * ids) for p in picked]
    weights = jnp.stack([jnp.sum(p).astype(jnp.float32) / members for p in picked])

    padded = jnp.pad(estimate, ((0, 0), (lead, lead), (0, 0)))
    windows = jnp.stack([padded[:, j * py : j * py + ext] for j in range(blocks)])
    pencil = lax.all_to_all(windows, "blk", 0, 0, tiled=True).reshape(nz, ext, nx)

    pick = lambda a: jnp.stack([lax.dynamic_index_in_dim(a, c, 0, keepdims=False) for c in chosen])
    pieces, planes, strips = pick(measured), pick(tile_plane), pick(tile_strip)
    hits = (strips[:, :, None] == jnp.arange(blocks, dtype=jnp.int32)).astype(jnp.int32)
    before = jnp.cumsum(hits, axis=1) - hits
    positions = strips * per + jnp.sum(before * hits, axis=2)
    order = positions[:, None, :] == jnp.arange(tiles, dtype=jnp.int32)[None, :, None]
    send_planes = jnp.sum(jnp.where(order, planes[:, None, :], 0), axis=2)
    send = jnp.einsum("vpi,viyx->pvyx", order.astype(jnp.bfloat16), pieces)
    got = lax.all_to_all(send, "blk", 0, 0, tiled=True)
    got_planes = lax.all_to_all(send_planes.T, "blk", 0, 0, tiled=True)
    place = (got_planes[None] == jnp.arange(nz, dtype=jnp.int32)[:, None, None]).astype(jnp.bfloat16)
    observed = jnp.einsum("ptv,tvyx->vpyx", place, got).astype(jnp.float32)

    kc, kr, kp = pick(kernel_cols), pick(kernel_rows), pick(kernel_planes)
    flat = lambda k: k.reshape(-1, k.shape[-1])
    fold = lambda m: m.reshape((VSLOT, -1) + m.shape[1:])
    bx, by, bz = map(fold, bands([(flat(kc), nx, nx, 0), (flat(kr), py, ext, lead), (flat(kp), nz, nz, 0)]))
    byw = by * weights[:, None, None, None]

    t = jnp.einsum("zmx,vrim->vrzix", pencil, by, precision=HIGH)
    t = jnp.einsum("vrzix,vrnx->vrzin", t, bx, precision=HIGH)
    blurred = jnp.einsum("vrzin,vrpz->vpin", t, bz, precision=HIGH)
    ratios = observed / blurred
    a = jnp.einsum("vpin,vrpz->vrzin", ratios, bz, precision=HIGH)
    a = jnp.einsum("vrzin,vrnx->vrzix", a, bx, precision=HIGH)
    wide = jnp.einsum("vrzix,vrim->zmx", a, byw, precision=HIGH)

    chunk = min(py, lead)
    average = wide[:, lead : lead + py]
    for d in range(1, lead // chunk + 1):
        up = wide[:, lead + py + (d - 1) * chunk : lead + py + d * chunk]
        down = wide[:, lead - d * chunk : lead - (d - 1) * chunk]
        up = lax.ppermute(up, "blk", [(i, i + d) for i in range(blocks - d)])
        down = lax.ppermute(down, "blk", [(i, i - d) for i in range(d, blocks)])
        rest = py - chunk
        average = average + jnp.pad(up, ((0, 0), (0, rest), (0, 0))) + jnp.pad(down, ((0, 0), (rest, 0), (0, 0)))
    logs = jnp.log(average)
    return finish(logs, estimate, blocks, groups)


def solution(mesh):
    in_specs = (
        P("blk", None, None),
        P(None, "blk", None, None),
        P(None, "blk"),
        P(None, "blk"),
        P(),
        P(),
        P(),
        P(),
    )
    return jax.shard_map(
        shards, mesh=mesh, in_specs=in_specs, out_specs=P("blk", None, None), check_vma=False
    )
```

```python
import jax
import jax.numpy as jnp
from jax import lax
from jax.experimental import pallas as pl
from jax.experimental.pallas import tpu as pltpu
from jax.sharding import PartitionSpec as P

VSLOT = 2
HIGH = lax.Precision.HIGH


MESH = pl.DeviceIdType.MESH


def band_kernel(*refs):
    count = len(refs) // 2
    for row, out in zip(refs[:count], refs[count:]):
        number, rows, cols = out.shape
        for n in range(number):
            wide = jnp.broadcast_to(row[n], (rows, row.shape[-1]))
            wide = pltpu.roll(wide, 0, 1, stride=1, stride_axis=0)
            out[n] = wide[:, :cols]


def bands(shapes):
    rows_in, outs = [], []
    for taps, rows, cols, lead in shapes:
        number, width = taps.shape
        half = width // 2
        span = -(-(max(cols, rows) + lead + width) // 128) * 128
        row = jnp.pad(taps, ((0, 0), (0, span - width)))
        row = jnp.roll(row, lead - half, axis=1)
        rows_in.append(row[:, None, :])
        outs.append(jax.ShapeDtypeStruct((number, rows, cols), jnp.float32))
    vmem = pl.BlockSpec(memory_space=pltpu.VMEM)
    return pl.pallas_call(
        band_kernel,
        out_shape=outs,
        in_specs=[vmem] * len(outs),
        out_specs=[vmem] * len(outs),
    )(*rows_in)


def spread_kernel(blocks, groups, step, padded, planes, pencil, got, sa, ra, sb, rb, sp, rp):
    me = lax.axis_index("blk")
    grp = lax.axis_index("grp")
    cz, span = pencil.shape[1], pencil.shape[2]
    cq = cz // groups
    mine = pl.ds(grp * cq, cq)
    barrier = pltpu.get_barrier_semaphore()
    for k in range(1, groups):
        pl.semaphore_signal(barrier, inc=1, device_id=(lax.rem(grp + k, groups), me), device_id_type=MESH)
    for rel in range(1, blocks):
        pl.semaphore_signal(barrier, inc=1, device_id=(grp, lax.rem(me + rel, blocks)), device_id_type=MESH)
    pl.semaphore_wait(barrier, groups + blocks - 2)

    first, small, second = {}, {}, {}
    for rel in range(1, blocks):
        dest = lax.rem(me + rel, blocks)
        first[rel] = pltpu.make_async_remote_copy(
            src_ref=padded.at[mine, pl.ds(dest * step, span)],
            dst_ref=pencil.at[me, mine],
            send_sem=sa.at[rel],
            recv_sem=ra.at[rel],
            device_id=(grp, dest),
            device_id_type=MESH,
        )
        first[rel].start()
    for rel in range(1, blocks):
        dest = lax.rem(me + rel, blocks)
        small[rel] = pltpu.make_async_remote_copy(
            src_ref=planes.at[dest],
            dst_ref=got.at[me],
            send_sem=sp.at[rel],
            recv_sem=rp.at[rel],
            device_id=(grp, dest),
            device_id_type=MESH,
        )
        small[rel].start()
    pencil[me] = padded[:, pl.ds(me * step, span)]
    got[me] = planes[me]
    for rel in range(1, blocks):
        src = lax.rem(me + blocks - rel, blocks)
        landed = pencil.at[src, mine]
        pltpu.make_async_remote_copy(
            src_ref=landed,
            dst_ref=landed,
            send_sem=sa.at[rel],
            recv_sem=ra.at[rel],
            device_id=(grp, src),
            device_id_type=MESH,
        ).wait_recv()
        for k in range(1, groups):
            second[rel, k] = pltpu.make_async_remote_copy(
                src_ref=landed,
                dst_ref=landed,
                send_sem=sb.at[rel, k - 1],
                recv_sem=rb.at[rel, k - 1],
                device_id=(lax.rem(grp + k, groups), me),
                device_id_type=MESH,
            )
            second[rel, k].start()
    for rel in range(1, blocks):
        src = lax.rem(me + blocks - rel, blocks)
        for k in range(1, groups):
            peer = lax.rem(grp + groups - k, groups)
            theirs = pencil.at[src, pl.ds(peer * cq, cq)]
            pltpu.make_async_remote_copy(
                src_ref=theirs,
                dst_ref=theirs,
                send_sem=sb.at[rel, k - 1],
                recv_sem=rb.at[rel, k - 1],
                device_id=(peer, me),
                device_id_type=MESH,
            ).wait_recv()
        pltpu.make_async_remote_copy(
            src_ref=planes.at[src],
            dst_ref=got.at[src],
            send_sem=sp.at[rel],
            recv_sem=rp.at[rel],
            device_id=(grp, src),
            device_id_type=MESH,
        ).wait_recv()
    for copies in (first, small, second):
        for copy in copies.values():
            copy.wait_send()


def spread(estimate, planes, lead, blocks, groups):
    cz, ny, nx = estimate.shape
    py = ny // blocks
    chunk = min(py, lead)
    span = (py + 2 * lead) // chunk
    padded = jnp.pad(estimate, ((0, 0), (lead, lead), (0, 0))).reshape(cz, -1, chunk, nx)
    vmem = pl.BlockSpec(memory_space=pltpu.VMEM)
    dma = pltpu.SemaphoreType.DMA
    pencil, got = pl.pallas_call(
        lambda *refs: spread_kernel(blocks, groups, py // chunk, *refs),
        out_shape=[
            jax.ShapeDtypeStruct((blocks, cz, span, chunk, nx), jnp.float32),
            jax.ShapeDtypeStruct(planes.shape, jnp.int32),
        ],
        in_specs=[vmem, vmem],
        out_specs=[vmem, vmem],
        scratch_shapes=[
            dma((blocks,)),
            dma((blocks,)),
            dma((blocks, groups - 1)),
            dma((blocks, groups - 1)),
            dma((blocks,)),
            dma((blocks,)),
        ],
        compiler_params=pltpu.CompilerParams(collective_id=1, has_side_effects=True),
        cost_estimate=pl.CostEstimate(flops=0, bytes_accessed=1 << 26, transcendentals=0),
        name="spread",
    )(padded, planes)
    return pencil.reshape(cz * blocks, py + 2 * lead, nx), got


def finish_kernel(blocks, groups, logs, est, out, got1, send2, got2, s1, r1, s2, r2, s3, r3):
    me = lax.axis_index("blk")
    grp = lax.axis_index("grp")
    cq = est.shape[0] // groups
    mine = pl.ds(grp * cq, cq)
    barrier = pltpu.get_barrier_semaphore()
    for k in range(1, groups):
        pl.semaphore_signal(barrier, inc=1, device_id=(lax.rem(grp + k, groups), me), device_id_type=MESH)
    for rel in range(1, blocks):
        pl.semaphore_signal(barrier, inc=1, device_id=(grp, lax.rem(me + rel, blocks)), device_id_type=MESH)
    pl.semaphore_wait(barrier, groups + blocks - 2)
    order = list(range(1, blocks)) + [0]

    first, second, third = {}, {}, {}
    for rel in order:
        dest = lax.rem(me + rel, blocks)
        for k in range(1, groups):
            peer = lax.rem(grp + k, groups)
            first[rel, k] = pltpu.make_async_remote_copy(
                src_ref=logs.at[dest, pl.ds(peer * cq, cq)],
                dst_ref=got1.at[rel, k - 1],
                send_sem=s1.at[rel, k - 1],
                recv_sem=r1.at[rel, k - 1],
                device_id=(peer, me),
                device_id_type=MESH,
            )
            first[rel, k].start()
    for rel in order:
        dest = lax.rem(me + rel, blocks)
        total = logs[dest, mine]
        for k in range(1, groups):
            first[rel, k].wait_recv()
            total = total + got1[rel, k - 1]
        if rel == 0:
            got2[0] = total
        else:
            send2[rel] = total
            second[rel] = pltpu.make_async_remote_copy(
                src_ref=send2.at[rel],
                dst_ref=got2.at[rel],
                send_sem=s2.at[rel],
                recv_sem=r2.at[rel],
                device_id=(grp, dest),
                device_id_type=MESH,
            )
            second[rel].start()
    for rel in order:
        strip = lax.rem(me + blocks - rel, blocks)
        if rel != 0:
            second[rel].wait_recv()
        out[mine, strip] = est[mine, strip] * jnp.exp(got2[rel] * (1.0 / groups))
        for k in range(1, groups):
            third[rel, k] = pltpu.make_async_remote_copy(
                src_ref=out.at[mine, strip],
                dst_ref=out.at[mine, strip],
                send_sem=s3.at[rel, k - 1],
                recv_sem=r3.at[rel, k - 1],
                device_id=(lax.rem(grp + k, groups), me),
                device_id_type=MESH,
            )
            third[rel, k].start()
    for copy in first.values():
        copy.wait_send()
    for copy in second.values():
        copy.wait_send()
    for copy in third.values():
        copy.wait_send()
    for rel in order:
        strip = lax.rem(me + blocks - rel, blocks)
        for k in range(1, groups):
            peer = lax.rem(grp + groups - k, groups)
            theirs = out.at[pl.ds(peer * cq, cq), strip]
            pltpu.make_async_remote_copy(
                src_ref=theirs,
                dst_ref=theirs,
                send_sem=s3.at[rel, k - 1],
                recv_sem=r3.at[rel, k - 1],
                device_id=(peer, me),
                device_id_type=MESH,
            ).wait_recv()


def finish(logs, estimate, blocks, groups):
    cz, ny, nx = estimate.shape
    py = ny // blocks
    cq = cz // groups
    vmem = pl.BlockSpec(memory_space=pltpu.VMEM)
    dma = pltpu.SemaphoreType.DMA
    out = pl.pallas_call(
        lambda *refs: finish_kernel(blocks, groups, *refs),
        out_shape=jax.ShapeDtypeStruct((cz, blocks, py, nx), jnp.float32),
        in_specs=[vmem, vmem],
        out_specs=vmem,
        scratch_shapes=[
            pltpu.VMEM((blocks, groups - 1, cq, py, nx), jnp.float32),
            pltpu.VMEM((blocks, cq, py, nx), jnp.float32),
            pltpu.VMEM((blocks, cq, py, nx), jnp.float32),
            dma((blocks, groups - 1)),
            dma((blocks, groups - 1)),
            dma((blocks,)),
            dma((blocks,)),
            dma((blocks, groups - 1)),
            dma((blocks, groups - 1)),
        ],
        compiler_params=pltpu.CompilerParams(collective_id=0, has_side_effects=True),
        name="finish",
    )(logs.reshape(blocks, cz, py, nx), estimate.reshape(cz, blocks, py, nx))
    return out.reshape(cz, ny, nx)


def shards(estimate, measured, tile_plane, tile_strip, view_group, kernel_cols, kernel_rows, kernel_planes):
    cz, ny, nx = estimate.shape
    blocks = lax.axis_size("blk")
    groups = lax.axis_size("grp")
    nz = cz * blocks
    py = ny // blocks
    half = kernel_rows.shape[-1] // 2
    lead = -(-half // 8) * 8
    ext = py + 2 * lead
    tiles = measured.shape[1]
    per = tiles // blocks

    matches = (view_group == lax.axis_index("grp")).astype(jnp.int32)
    ranking = jnp.cumsum(matches) - matches
    members = jnp.sum(matches).astype(jnp.float32)
    ids = jnp.arange(view_group.shape[0], dtype=jnp.int32)
    picked = [matches * (ranking == s).astype(jnp.int32) for s in range(VSLOT)]
    chosen = [jnp.sum(p * ids) for p in picked]
    weights = jnp.stack([jnp.sum(p).astype(jnp.float32) / members for p in picked])

    pick = lambda a: jnp.stack([lax.dynamic_index_in_dim(a, c, 0, keepdims=False) for c in chosen])
    pieces, planes, strips = pick(measured), pick(tile_plane), pick(tile_strip)
    hits = (strips[:, :, None] == jnp.arange(blocks, dtype=jnp.int32)).astype(jnp.int32)
    before = jnp.cumsum(hits, axis=1) - hits
    positions = strips * per + jnp.sum(before * hits, axis=2)
    order = positions[:, None, :] == jnp.arange(tiles, dtype=jnp.int32)[None, :, None]
    send_planes = jnp.sum(jnp.where(order, planes[:, None, :], 0), axis=2)
    send = jnp.einsum("vpi,viyx->pvyx", order.astype(jnp.bfloat16), pieces)
    got = lax.all_to_all(send, "blk", 0, 0, tiled=True)

    table = send_planes.reshape(VSLOT, blocks, per).transpose(1, 0, 2)
    table = jnp.pad(table, ((0, 0), (0, 8 - VSLOT), (0, 128 - per)))
    pencil, table = spread(estimate, table, lead, blocks, groups)
    got_planes = table[:, :VSLOT, :per].transpose(0, 2, 1).reshape(tiles, VSLOT)
    place = (got_planes[None] == jnp.arange(nz, dtype=jnp.int32)[:, None, None]).astype(jnp.bfloat16)
    observed = jnp.einsum("ptv,tvyx->vpyx", place, got).astype(jnp.float32)

    kc, kr, kp = pick(kernel_cols), pick(kernel_rows), pick(kernel_planes)
    flat = lambda k: k.reshape(-1, k.shape[-1])
    fold = lambda m: m.reshape((VSLOT, -1) + m.shape[1:])
    bx, by, bz = map(fold, bands([(flat(kc), nx, nx, 0), (flat(kr), py, ext, lead), (flat(kp), nz, nz, 0)]))
    byw = by * weights[:, None, None, None]

    t = jnp.einsum("zmx,vrim->vrzix", pencil, by, precision=HIGH)
    t = jnp.einsum("vrzix,vrnx->vrzin", t, bx, precision=HIGH)
    blurred = jnp.einsum("vrzin,vrpz->vpin", t, bz, precision=HIGH)
    ratios = observed / blurred
    a = jnp.einsum("vpin,vrpz->vrzin", ratios, bz, precision=HIGH)
    a = jnp.einsum("vrzin,vrnx->vrzix", a, bx, precision=HIGH)
    wide = jnp.einsum("vrzix,vrim->zmx", a, byw, precision=HIGH)

    chunk = min(py, lead)
    average = wide[:, lead : lead + py]
    for d in range(1, lead // chunk + 1):
        up = wide[:, lead + py + (d - 1) * chunk : lead + py + d * chunk]
        down = wide[:, lead - d * chunk : lead - (d - 1) * chunk]
        up = lax.ppermute(up, "blk", [(i, i + d) for i in range(blocks - d)])
        down = lax.ppermute(down, "blk", [(i, i - d) for i in range(d, blocks)])
        rest = py - chunk
        average = average + jnp.pad(up, ((0, 0), (0, rest), (0, 0))) + jnp.pad(down, ((0, 0), (rest, 0), (0, 0)))
    logs = jnp.log(average)
    return finish(logs, estimate, blocks, groups)


def solution(mesh):
    in_specs = (
        P("blk", None, None),
        P(None, "blk", None, None),
        P(None, "blk"),
        P(None, "blk"),
        P(),
        P(),
        P(),
        P(),
    )
    return jax.shard_map(
        shards, mesh=mesh, in_specs=in_specs, out_specs=P("blk", None, None), check_vma=False
    )
```

```python
import jax
import jax.numpy as jnp
from jax import lax
from jax.experimental import pallas as pl
from jax.experimental.pallas import tpu as pltpu
from jax.sharding import PartitionSpec as P

VSLOT = 2
HIGH = lax.Precision.HIGH


MESH = pl.DeviceIdType.MESH


def band_kernel(*refs):
    count = len(refs) // 2
    for row, out in zip(refs[:count], refs[count:]):
        number, rows, cols = out.shape
        for n in range(number):
            wide = jnp.broadcast_to(row[n], (rows, row.shape[-1]))
            wide = pltpu.roll(wide, 0, 1, stride=1, stride_axis=0)
            out[n] = wide[:, :cols]


def bands(shapes):
    rows_in, outs = [], []
    for taps, rows, cols, lead in shapes:
        number, width = taps.shape
        half = width // 2
        span = -(-(max(cols, rows) + lead + width) // 128) * 128
        row = jnp.pad(taps, ((0, 0), (0, span - width)))
        row = jnp.roll(row, lead - half, axis=1)
        rows_in.append(row[:, None, :])
        outs.append(jax.ShapeDtypeStruct((number, rows, cols), jnp.float32))
    vmem = pl.BlockSpec(memory_space=pltpu.VMEM)
    return pl.pallas_call(
        band_kernel,
        out_shape=outs,
        in_specs=[vmem] * len(outs),
        out_specs=[vmem] * len(outs),
    )(*rows_in)


def spread_kernel(blocks, groups, step, padded, planes, tiles, pencil, got, arrived, sa, ra, sb, rb, sp, rp, st, rt):
    me = lax.axis_index("blk")
    grp = lax.axis_index("grp")
    cz, span = pencil.shape[1], pencil.shape[2]
    cq = cz // groups
    mine = pl.ds(grp * cq, cq)
    barrier = pltpu.get_barrier_semaphore()
    for k in range(1, groups):
        pl.semaphore_signal(barrier, inc=1, device_id=(lax.rem(grp + k, groups), me), device_id_type=MESH)
    for rel in range(1, blocks):
        pl.semaphore_signal(barrier, inc=1, device_id=(grp, lax.rem(me + rel, blocks)), device_id_type=MESH)
    pl.semaphore_wait(barrier, groups + blocks - 2)

    first, small, second, large = {}, {}, {}, {}
    for rel in range(1, blocks):
        dest = lax.rem(me + rel, blocks)
        first[rel] = pltpu.make_async_remote_copy(
            src_ref=padded.at[mine, pl.ds(dest * step, span)],
            dst_ref=pencil.at[me, mine],
            send_sem=sa.at[rel],
            recv_sem=ra.at[rel],
            device_id=(grp, dest),
            device_id_type=MESH,
        )
        first[rel].start()
    for rel in range(1, blocks):
        dest = lax.rem(me + rel, blocks)
        small[rel] = pltpu.make_async_remote_copy(
            src_ref=planes.at[dest],
            dst_ref=got.at[me],
            send_sem=sp.at[rel],
            recv_sem=rp.at[rel],
            device_id=(grp, dest),
            device_id_type=MESH,
        )
        small[rel].start()
    for rel in range(1, blocks):
        dest = lax.rem(me + rel, blocks)
        large[rel] = pltpu.make_async_remote_copy(
            src_ref=tiles.at[dest],
            dst_ref=arrived.at[me],
            send_sem=st.at[rel],
            recv_sem=rt.at[rel],
            device_id=(grp, dest),
            device_id_type=MESH,
        )
        large[rel].start()
    arrived[me] = tiles[me]
    pencil[me] = padded[:, pl.ds(me * step, span)]
    got[me] = planes[me]
    for rel in range(1, blocks):
        src = lax.rem(me + blocks - rel, blocks)
        landed = pencil.at[src, mine]
        pltpu.make_async_remote_copy(
            src_ref=landed,
            dst_ref=landed,
            send_sem=sa.at[rel],
            recv_sem=ra.at[rel],
            device_id=(grp, src),
            device_id_type=MESH,
        ).wait_recv()
        for k in range(1, groups):
            second[rel, k] = pltpu.make_async_remote_copy(
                src_ref=landed,
                dst_ref=landed,
                send_sem=sb.at[rel, k - 1],
                recv_sem=rb.at[rel, k - 1],
                device_id=(lax.rem(grp + k, groups), me),
                device_id_type=MESH,
            )
            second[rel, k].start()
    for rel in range(1, blocks):
        src = lax.rem(me + blocks - rel, blocks)
        for k in range(1, groups):
            peer = lax.rem(grp + groups - k, groups)
            theirs = pencil.at[src, pl.ds(peer * cq, cq)]
            pltpu.make_async_remote_copy(
                src_ref=theirs,
                dst_ref=theirs,
                send_sem=sb.at[rel, k - 1],
                recv_sem=rb.at[rel, k - 1],
                device_id=(peer, me),
                device_id_type=MESH,
            ).wait_recv()
        pltpu.make_async_remote_copy(
            src_ref=planes.at[src],
            dst_ref=got.at[src],
            send_sem=sp.at[rel],
            recv_sem=rp.at[rel],
            device_id=(grp, src),
            device_id_type=MESH,
        ).wait_recv()
        pltpu.make_async_remote_copy(
            src_ref=tiles.at[src],
            dst_ref=arrived.at[src],
            send_sem=st.at[rel],
            recv_sem=rt.at[rel],
            device_id=(grp, src),
            device_id_type=MESH,
        ).wait_recv()
    for copies in (first, small, second, large):
        for copy in copies.values():
            copy.wait_send()


def spread(estimate, planes, tiles, lead, blocks, groups):
    cz, ny, nx = estimate.shape
    py = ny // blocks
    chunk = min(py, lead)
    span = (py + 2 * lead) // chunk
    padded = jnp.pad(estimate, ((0, 0), (lead, lead), (0, 0))).reshape(cz, -1, chunk, nx)
    vmem = pl.BlockSpec(memory_space=pltpu.VMEM)
    dma = pltpu.SemaphoreType.DMA
    pencil, got, arrived = pl.pallas_call(
        lambda *refs: spread_kernel(blocks, groups, py // chunk, *refs),
        out_shape=[
            jax.ShapeDtypeStruct((blocks, cz, span, chunk, nx), jnp.float32),
            jax.ShapeDtypeStruct(planes.shape, jnp.int32),
            jax.ShapeDtypeStruct(tiles.shape, tiles.dtype),
        ],
        in_specs=[vmem] * 3,
        out_specs=[vmem] * 3,
        scratch_shapes=[
            dma((blocks,)),
            dma((blocks,)),
            dma((blocks, groups - 1)),
            dma((blocks, groups - 1)),
            dma((blocks,)),
            dma((blocks,)),
            dma((blocks,)),
            dma((blocks,)),
        ],
        compiler_params=pltpu.CompilerParams(collective_id=1, has_side_effects=True),
        cost_estimate=pl.CostEstimate(flops=0, bytes_accessed=1 << 26, transcendentals=0),
        name="spread",
    )(padded, planes, tiles)
    return pencil.reshape(cz * blocks, py + 2 * lead, nx), got, arrived


def finish_kernel(blocks, groups, logs, est, out, got1, send2, got2, s1, r1, s2, r2, s3, r3):
    me = lax.axis_index("blk")
    grp = lax.axis_index("grp")
    cq = est.shape[0] // groups
    mine = pl.ds(grp * cq, cq)
    barrier = pltpu.get_barrier_semaphore()
    for k in range(1, groups):
        pl.semaphore_signal(barrier, inc=1, device_id=(lax.rem(grp + k, groups), me), device_id_type=MESH)
    for rel in range(1, blocks):
        pl.semaphore_signal(barrier, inc=1, device_id=(grp, lax.rem(me + rel, blocks)), device_id_type=MESH)
    pl.semaphore_wait(barrier, groups + blocks - 2)
    order = list(range(1, blocks)) + [0]

    first, second, third = {}, {}, {}
    for rel in order:
        dest = lax.rem(me + rel, blocks)
        for k in range(1, groups):
            peer = lax.rem(grp + k, groups)
            first[rel, k] = pltpu.make_async_remote_copy(
                src_ref=logs.at[dest, pl.ds(peer * cq, cq)],
                dst_ref=got1.at[rel, k - 1],
                send_sem=s1.at[rel, k - 1],
                recv_sem=r1.at[rel, k - 1],
                device_id=(peer, me),
                device_id_type=MESH,
            )
            first[rel, k].start()
    for rel in order:
        dest = lax.rem(me + rel, blocks)
        total = logs[dest, mine]
        for k in range(1, groups):
            first[rel, k].wait_recv()
            total = total + got1[rel, k - 1]
        if rel == 0:
            got2[0] = total
        else:
            send2[rel] = total
            second[rel] = pltpu.make_async_remote_copy(
                src_ref=send2.at[rel],
                dst_ref=got2.at[rel],
                send_sem=s2.at[rel],
                recv_sem=r2.at[rel],
                device_id=(grp, dest),
                device_id_type=MESH,
            )
            second[rel].start()
    for rel in order:
        strip = lax.rem(me + blocks - rel, blocks)
        if rel != 0:
            second[rel].wait_recv()
        out[mine, strip] = est[mine, strip] * jnp.exp(got2[rel] * (1.0 / groups))
        for k in range(1, groups):
            third[rel, k] = pltpu.make_async_remote_copy(
                src_ref=out.at[mine, strip],
                dst_ref=out.at[mine, strip],
                send_sem=s3.at[rel, k - 1],
                recv_sem=r3.at[rel, k - 1],
                device_id=(lax.rem(grp + k, groups), me),
                device_id_type=MESH,
            )
            third[rel, k].start()
    for copy in first.values():
        copy.wait_send()
    for copy in second.values():
        copy.wait_send()
    for copy in third.values():
        copy.wait_send()
    for rel in order:
        strip = lax.rem(me + blocks - rel, blocks)
        for k in range(1, groups):
            peer = lax.rem(grp + groups - k, groups)
            theirs = out.at[pl.ds(peer * cq, cq), strip]
            pltpu.make_async_remote_copy(
                src_ref=theirs,
                dst_ref=theirs,
                send_sem=s3.at[rel, k - 1],
                recv_sem=r3.at[rel, k - 1],
                device_id=(peer, me),
                device_id_type=MESH,
            ).wait_recv()


def finish(logs, estimate, blocks, groups):
    cz, ny, nx = estimate.shape
    py = ny // blocks
    cq = cz // groups
    vmem = pl.BlockSpec(memory_space=pltpu.VMEM)
    dma = pltpu.SemaphoreType.DMA
    out = pl.pallas_call(
        lambda *refs: finish_kernel(blocks, groups, *refs),
        out_shape=jax.ShapeDtypeStruct((cz, blocks, py, nx), jnp.float32),
        in_specs=[vmem, vmem],
        out_specs=vmem,
        scratch_shapes=[
            pltpu.VMEM((blocks, groups - 1, cq, py, nx), jnp.float32),
            pltpu.VMEM((blocks, cq, py, nx), jnp.float32),
            pltpu.VMEM((blocks, cq, py, nx), jnp.float32),
            dma((blocks, groups - 1)),
            dma((blocks, groups - 1)),
            dma((blocks,)),
            dma((blocks,)),
            dma((blocks, groups - 1)),
            dma((blocks, groups - 1)),
        ],
        compiler_params=pltpu.CompilerParams(collective_id=0, has_side_effects=True),
        name="finish",
    )(logs.reshape(blocks, cz, py, nx), estimate.reshape(cz, blocks, py, nx))
    return out.reshape(cz, ny, nx)


def shards(estimate, measured, tile_plane, tile_strip, view_group, kernel_cols, kernel_rows, kernel_planes):
    cz, ny, nx = estimate.shape
    blocks = lax.axis_size("blk")
    groups = lax.axis_size("grp")
    nz = cz * blocks
    py = ny // blocks
    half = kernel_rows.shape[-1] // 2
    lead = -(-half // 8) * 8
    ext = py + 2 * lead
    tiles = measured.shape[1]
    per = tiles // blocks

    matches = (view_group == lax.axis_index("grp")).astype(jnp.int32)
    members = jnp.sum(matches).astype(jnp.float32)
    ids = jnp.arange(view_group.shape[0], dtype=jnp.int32)
    ranking = jnp.sum(jnp.where(ids[None, :] < ids[:, None], matches[None, :], 0), axis=1)
    picked = [matches * (ranking == s).astype(jnp.int32) for s in range(VSLOT)]
    chosen = [jnp.sum(p * ids) for p in picked]
    weights = jnp.stack([jnp.sum(p).astype(jnp.float32) / members for p in picked])

    pick = lambda a: jnp.stack([lax.dynamic_index_in_dim(a, c, 0, keepdims=False) for c in chosen])
    pieces, planes, strips = pick(measured), pick(tile_plane), pick(tile_strip)
    number = jnp.arange(tiles, dtype=jnp.int32)
    earlier = (strips[:, :, None] == strips[:, None, :]) & (number[None, :] < number[:, None])
    positions = strips * per + jnp.sum(earlier.astype(jnp.int32), axis=2)
    order = positions[:, None, :] == jnp.arange(tiles, dtype=jnp.int32)[None, :, None]
    send_planes = jnp.sum(jnp.where(order, planes[:, None, :], 0), axis=2)
    send = jnp.einsum("vpi,viyx->pvyx", order.astype(jnp.bfloat16), pieces)
    send = send.reshape(blocks, per, VSLOT, py, nx)

    table = send_planes.reshape(VSLOT, blocks, per).transpose(1, 0, 2)
    table = jnp.pad(table, ((0, 0), (0, 8 - VSLOT), (0, 128 - per)))
    pencil, table, got = spread(estimate, table, send, lead, blocks, groups)
    got = got.reshape(tiles, VSLOT, py, nx)
    got_planes = table[:, :VSLOT, :per].transpose(0, 2, 1).reshape(tiles, VSLOT)
    place = (got_planes[None] == jnp.arange(nz, dtype=jnp.int32)[:, None, None]).astype(jnp.bfloat16)
    observed = jnp.einsum("ptv,tvyx->vpyx", place, got).astype(jnp.float32)

    kc, kr, kp = pick(kernel_cols), pick(kernel_rows), pick(kernel_planes)
    flat = lambda k: k.reshape(-1, k.shape[-1])
    fold = lambda m: m.reshape((VSLOT, -1) + m.shape[1:])
    bx, by, bz = map(fold, bands([(flat(kc), nx, nx, 0), (flat(kr), py, ext, lead), (flat(kp), nz, nz, 0)]))
    byw = by * weights[:, None, None, None]

    t = jnp.einsum("zmx,vrim->vrzix", pencil, by, precision=HIGH)
    t = jnp.einsum("vrzix,vrnx->vrzin", t, bx, precision=HIGH)
    blurred = jnp.einsum("vrzin,vrpz->vpin", t, bz, precision=HIGH)
    ratios = observed / blurred
    a = jnp.einsum("vpin,vrpz->vrzin", ratios, bz, precision=HIGH)
    a = jnp.einsum("vrzin,vrnx->vrzix", a, bx, precision=HIGH)
    wide = jnp.einsum("vrzix,vrim->zmx", a, byw, precision=HIGH)

    chunk = min(py, lead)
    average = wide[:, lead : lead + py]
    for d in range(1, lead // chunk + 1):
        up = wide[:, lead + py + (d - 1) * chunk : lead + py + d * chunk]
        down = wide[:, lead - d * chunk : lead - (d - 1) * chunk]
        up = lax.ppermute(up, "blk", [(i, i + d) for i in range(blocks - d)])
        down = lax.ppermute(down, "blk", [(i, i - d) for i in range(d, blocks)])
        rest = py - chunk
        average = average + jnp.pad(up, ((0, 0), (0, rest), (0, 0))) + jnp.pad(down, ((0, 0), (rest, 0), (0, 0)))
    logs = jnp.log(average)
    return finish(logs, estimate, blocks, groups)


def solution(mesh):
    in_specs = (
        P("blk", None, None),
        P(None, "blk", None, None),
        P(None, "blk"),
        P(None, "blk"),
        P(),
        P(),
        P(),
        P(),
    )
    return jax.shard_map(
        shards, mesh=mesh, in_specs=in_specs, out_specs=P("blk", None, None), check_vma=False
    )
```
